256 devices in a mesh: row: 16 (over x_hi, y, core), col: 16 (over z, x_lo).
Axes of the slice: x: 4 (x_hi: 2, x_lo: 2; x = x_hi * 2 + x_lo), y: 4, z: 8, core: 2. Of those that a mesh axis runs over, the one named last changes fastest.
Arguments:
- inputs: bfloat16 [2048, 4096], P('row', 'col'), may hold values from -6 to 6
- grad_output: bfloat16 [2048, 4096], P('row', 'col'), may hold values from -6 to 6
- gate_pre: bfloat16 [2048, 14336], P('col', 'row'), may hold values from -6 to 6
- up_pre: bfloat16 [2048, 14336], P('col', 'row'), may hold values from -6 to 6
- gate_weight: bfloat16 [14336, 4096], P('row', 'col'), may hold values from -0.09375 to 0.09375
- up_weight: bfloat16 [14336, 4096], P('row', 'col'), may hold values from -0.09375 to 0.09375
- down_weight: bfloat16 [14336, 4096], P('row', 'col'), may hold values from -0.046875 to 0.046875
Outputs:
- grad_input: float32 [2048, 4096], P('row', 'col')
- grad_gate_weight: float32 [14336, 4096], P('row', 'col')
- grad_up_weight: float32 [14336, 4096], P('row', 'col')
- grad_down_weight: float32 [14336, 4096], P('row', 'col')
The draws below stay inside these ranges and needn't reach their ends.
All inputs are finite; a program needn't handle non-finite values.
Results may differ from the reference program's by a relative error of at most 0.0029.
Values may be sent and summed in bfloat16 or wider, within the bound.
No kernel may reach another device: no remote copies, remote signals or barrier semaphores. Data moves between devices by JAX's collectives and lax.ppermute only.
A program may use at most 64 MiB of HBM per device.

```python
import math
import jax
import jax.numpy as jnp

D = 4096
FF = 14336
TOKENS = 2048


def with_spikes(values, stream_key, source, target, parts, factor):
    def block_of(dim):
        return (jnp.arange(values.shape[dim]) // (values.shape[dim] // parts)).reshape((-1,) + (1,) * (values.ndim - 1 - dim))

    one_side = jax.random.permutation(stream_key, parts)[block_of(target)]
    second = (block_of(target) + parts // 2) % parts
    return jnp.where((block_of(source) == one_side) | (block_of(source) == second), factor * values, values)


def shard_levels(own_key, shape, shards, smallest, largest):
    loudness = 1.0
    for dim, shards_of in shards:
        draws = jax.random.uniform(jax.random.fold_in(jax.random.fold_in(own_key, 6), dim), (shards_of,), jnp.float32, smallest / len(shards), largest / len(shards))
        loudness = loudness * jnp.repeat(jnp.exp(draws), shape[dim] // shards_of).reshape((-1,) + (1,) * (len(shape) - 1 - dim))
    return loudness


def bell_draw(own_key, extent, width, limit, cuts=(), dtype=jnp.bfloat16):
    entries = width * jax.random.normal(own_key, extent, jnp.float32)
    if cuts:
        entries = entries * shard_levels(own_key, extent, cuts, -0.22, 0.18)
    return jnp.clip(entries, -limit, limit).astype(dtype)


def noise_with(rng, shape, spread, limit, split, heavy, held_as=jnp.bfloat16):
    drawn = spread * jax.random.normal(rng, shape, jnp.float32)
    if split:
        drawn = drawn * shard_levels(rng, shape, split, -0.22, 0.18)
    return jnp.clip(with_spikes(drawn, jax.random.fold_in(rng, 3), *heavy), -limit, limit).astype(held_as)


def setup_inputs(seed: int = 0) -> dict:
    key_list = jax.random.split(jax.random.key(seed), 8)
    return {
        "inputs": bell_draw(key_list[0], (TOKENS, D), 1.0, 6.0, ((0, 16), (1, 16))),
        "grad_output": noise_with(key_list[1], (TOKENS, D), 1.0, 6.0, ((0, 16), (1, 16)), (1, 0, 16, 2.0)),
        "gate_pre": bell_draw(key_list[2], (TOKENS, FF), 1.0, 6.0, ((0, 16), (1, 16))),
        "up_pre": noise_with(key_list[3], (TOKENS, FF), 1.0, 6.0, ((0, 16), (1, 16)), (1, 0, 16, 2.0)),
        "gate_weight": bell_draw(key_list[4], (FF, D), D ** -0.5, 0.09375, ((0, 16), (1, 16))),
        "up_weight": bell_draw(key_list[5], (FF, D), D ** -0.5, 0.09375, ((0, 16), (1, 16))),
        "down_weight": bell_draw(key_list[6], (FF, D), FF ** -0.5, 0.046875, ((0, 16), (1, 16))),
    }


def reference(inputs, grad_output, gate_pre, up_pre, gate_weight, up_weight, down_weight):
    gate_value = gate_pre.astype(jnp.float32)
    up_value = up_pre.astype(jnp.float32)
    sigmoid_gate = jax.nn.sigmoid(gate_value)
    silu_gate = gate_value * sigmoid_gate
    hidden = (silu_gate * up_value).astype(jnp.bfloat16)
    grad_hidden = jnp.dot(grad_output, down_weight.T, preferred_element_type=jnp.float32)
    grad_gate_pre = (grad_hidden * up_value * sigmoid_gate * (1.0 + gate_value * (1.0 - sigmoid_gate))).astype(jnp.bfloat16)
    grad_up_pre = (grad_hidden * silu_gate).astype(jnp.bfloat16)
    grad_input = jnp.dot(grad_gate_pre, gate_weight, preferred_element_type=jnp.float32) + jnp.dot(grad_up_pre, up_weight, preferred_element_type=jnp.float32)
    factor = 1.0 / math.sqrt(TOKENS)
    grad_gate_weight = jnp.dot(grad_gate_pre.T, inputs, preferred_element_type=jnp.float32) * factor
    grad_up_weight = jnp.dot(grad_up_pre.T, inputs, preferred_element_type=jnp.float32) * factor
    grad_down_weight = jnp.dot(hidden.T, grad_output, preferred_element_type=jnp.float32) * factor
    return (grad_input, grad_gate_weight, grad_up_weight, grad_down_weight)
```

```python
import math

import jax
import jax.numpy as jnp
from jax import lax
from jax.sharding import Mesh, PartitionSpec as P

F32 = jnp.float32
BF16 = jnp.bfloat16


def shift(value, axis, size, by):
    return lax.ppermute(value, axis, [(i, (i + by) % size) for i in range(size)])


def dot(left, right, left_dim, right_dim):
    return lax.dot_general(
        left, right, (((left_dim,), (right_dim,)), ((), ())), preferred_element_type=F32
    )


def gather_rows(block, is_first):
    ring = ("xh", "xl")
    half = block.shape[0] // 2
    from_right = shift(block, ring, 4, -1)
    from_left = shift(block, ring, 4, 1)
    far = jnp.concatenate(
        [shift(from_left[:half], ring, 4, 1), shift(from_right[half:], ring, 4, -1)], axis=0
    )
    same = jnp.where(is_first, from_right, from_left)
    other = jnp.where(is_first, from_left, from_right)
    here = jnp.stack(
        [jnp.concatenate([block, same], axis=1), jnp.concatenate([far, other], axis=1)]
    )
    up = shift(here, "y", 4, -1)
    down = shift(here, "y", 4, 1)
    across = jnp.concatenate(
        [shift(down[:, :half], "y", 4, 1), shift(up[:, half:], "y", 4, -1)], axis=1
    )
    mine = jnp.stack([here, up, across, down], axis=1)
    return jnp.concatenate([mine, shift(mine, "core", 2, 1)], axis=2)


def swap_units(weight, which):
    half = weight.shape[0] // 2
    keep = lax.dynamic_slice_in_dim(weight, which * half, half, 0)
    give = lax.dynamic_slice_in_dim(weight, (1 - which) * half, half, 0)
    return jnp.concatenate([keep, shift(give, "xl", 2, 1)], axis=1)


def swap_tokens(hidden_rows, which, mine_first):
    turned = hidden_rows.T
    half = turned.shape[0] // 2
    keep = lax.dynamic_slice_in_dim(turned, which * half, half, 0)
    give = lax.dynamic_slice_in_dim(turned, (1 - which) * half, half, 0)
    got = shift(give, "xl", 2, 1)
    return jnp.where(
        mine_first,
        jnp.concatenate([keep, got], axis=1),
        jnp.concatenate([got, keep], axis=1),
    )


def gather_z(block):
    half = block.shape[1] // 2
    right, left = [block], [block]
    for _ in range(3):
        right.append(shift(right[-1], "z", 8, 1))
        left.append(shift(left[-1], "z", 8, -1))
    far = jnp.concatenate(
        [shift(right[3][:, :half], "z", 8, 1), shift(left[3][:, half:], "z", 8, -1)], axis=1
    )
    return [block, left[1], left[2], left[3], far, right[3], right[2], right[1]]


def shards(inputs, grad_output, gate_pre, up_pre, gate_weight, up_weight, down_weight):
    xh, y, core = lax.axis_index("xh"), lax.axis_index("y"), lax.axis_index("core")
    z, xl = lax.axis_index("z"), lax.axis_index("xl")
    is_first = xl == 0
    tokens = inputs.shape[0] * 16
    factor = 1.0 / math.sqrt(tokens)

    def chunk_of(rows, by):
        j = (z + by) % 8
        start = ((j // 4 - xh) % 2, (j % 4 - y) % 4, 0, 0)
        return lax.dynamic_slice(rows, start, (1, 1) + rows.shape[2:]).reshape(rows.shape[2:])

    down_units = swap_units(down_weight, xl)
    output_rows = gather_rows(grad_output, is_first)

    def part(by):
        return dot(down_units, chunk_of(output_rows, by), 1, 1)

    gate_value = swap_tokens(gate_pre, xl, xl == core).astype(F32)
    up_value = swap_tokens(up_pre, xl, xl == core).astype(F32)
    sigmoid_gate = jax.nn.sigmoid(gate_value)
    silu_gate = gate_value * sigmoid_gate
    hidden = (silu_gate * up_value).astype(BF16)
    hidden_blocks = gather_z(hidden)

    far = part(4)
    right = shift(far[:, :128], "z", 8, 1)
    left = shift(far[:, 128:], "z", 8, -1)
    three, back = part(3), part(-3)
    right = shift(jnp.concatenate([three[:, :128] + right, three[:, 128:]], axis=1), "z", 8, 1)
    left = shift(jnp.concatenate([back[:, :128], back[:, 128:] + left], axis=1), "z", 8, -1)
    for by in (2, 1):
        right = shift(part(by) + right, "z", 8, 1)
        left = shift(part(-by) + left, "z", 8, -1)
    grad_hidden = part(0) + right + left

    grad_gate_pre = (
        grad_hidden * up_value * sigmoid_gate * (1.0 + gate_value * (1.0 - sigmoid_gate))
    ).astype(BF16)
    grad_up_pre = (grad_hidden * silu_gate).astype(BF16)
    both = jnp.concatenate([grad_gate_pre, grad_up_pre], axis=0)
    both_blocks = gather_z(both)

    input_rows = gather_rows(inputs, is_first)
    both_units = jnp.concatenate(
        [swap_units(gate_weight, xl), swap_units(up_weight, xl)], axis=0
    )

    def weights_of(blocks, rows):
        total = None
        for by in (0, 1, 7, 2, 6, 3, 5, 4):
            term = dot(blocks[by], chunk_of(rows, by), 1, 0)
            total = term if total is None else total + term
        return total * factor

    def settle(grad):
        mid = grad.shape[1] // 2
        keep, got = grad[:, :mid], shift(grad[:, mid:], "xl", 2, 1)
        return jnp.where(
            is_first,
            jnp.concatenate([keep, got], axis=0),
            jnp.concatenate([got, keep], axis=0),
        )

    grad_down = settle(weights_of(hidden_blocks, output_rows))

    partial_input = jnp.stack([dot(block, both_units, 0, 0) for block in both_blocks])
    lanes = partial_input.shape[2] // 2
    summed = partial_input[:, :128] + shift(partial_input[:, 128:], "core", 2, 1)

    def toward(xr, yr):
        j = ((xh + xr) % 2) * 4 + (y + yr) % 4
        return lax.dynamic_slice_in_dim(summed, (j - z) % 8, 1, 0)

    def toward_y(yr):
        return jnp.concatenate([toward(0, yr), toward(1, yr)], axis=0)

    across = toward_y(2)
    a, b = shift(across[:, :64], "y", 4, 1), shift(across[:, 64:], "y", 4, -1)
    one, three = toward_y(1), toward_y(3)
    one = jnp.concatenate([one[:, :64] + a, one[:, 64:]], axis=1)
    three = jnp.concatenate([three[:, :64], three[:, 64:] + b], axis=1)
    summed_y = toward_y(0) + shift(one, "y", 4, 1) + shift(three, "y", 4, -1)

    ring = ("xh", "xl")
    near, beyond = summed_y[0, :, lanes:], summed_y[1, :, lanes:]
    opposite = summed_y[1, :, :lanes]
    a, b = shift(opposite[:64], ring, 4, 1), shift(opposite[64:], ring, 4, -1)
    one = jnp.where(is_first, near, beyond)
    three = jnp.where(is_first, beyond, near)
    one = jnp.concatenate([one[:64] + a, one[64:]], axis=0)
    three = jnp.concatenate([three[:64], three[64:] + b], axis=0)
    grad_input = summed_y[0, :, :lanes] + shift(one, ring, 4, 1) + shift(three, ring, 4, -1)

    grad_both = weights_of(both_blocks, input_rows)
    units = grad_both.shape[0] // 2
    mid = grad_both.shape[1] // 2
    keep, got = grad_both[:, :mid], shift(grad_both[:, mid:], "xl", 2, 1)

    def ordered(rows):
        return jnp.where(
            is_first,
            jnp.concatenate([keep[rows], got[rows]], axis=0),
            jnp.concatenate([got[rows], keep[rows]], axis=0),
        )

    grad_gate = ordered(slice(0, units))
    grad_up = ordered(slice(units, 2 * units))
    return grad_input, grad_gate, grad_up, grad_down


def solution(mesh):
    fine = Mesh(mesh.devices.reshape(2, 4, 2, 8, 2), ("xh", "y", "core", "z", "xl"))
    rows_cols = P(("xh", "y", "core"), ("z", "xl"))
    cols_rows = P(("z", "xl"), ("xh", "y", "core"))
    return jax.shard_map(
        shards,
        mesh=fine,
        in_specs=(rows_cols, rows_cols, cols_rows, cols_rows, rows_cols, rows_cols, rows_cols),
        out_specs=(rows_cols,) * 4,
        check_vma=False,
    )
```

```python
import math

import jax
import jax.numpy as jnp
from jax import lax
from jax.sharding import Mesh, PartitionSpec as P

F32 = jnp.float32
BF16 = jnp.bfloat16


def shift(value, axis, size, by):
    return lax.ppermute(value, axis, [(i, (i + by) % size) for i in range(size)])


def dot(left, right, left_dim, right_dim):
    return lax.dot_general(
        left, right, (((left_dim,), (right_dim,)), ((), ())), preferred_element_type=F32
    )


def after(value, *others):
    return lax.optimization_barrier((value,) + others)[0]


def gather_x(block, is_first):
    ring = ("xh", "xl")
    half = block.shape[0] // 2
    from_right = shift(block, ring, 4, -1)
    from_left = shift(block, ring, 4, 1)
    far = jnp.concatenate(
        [shift(from_left[:half], ring, 4, 1), shift(from_right[half:], ring, 4, -1)], axis=0
    )
    same = jnp.where(is_first, from_right, from_left)
    other = jnp.where(is_first, from_left, from_right)
    return jnp.stack(
        [jnp.concatenate([block, same], axis=1), jnp.concatenate([far, other], axis=1)]
    )


def gather_y(here):
    half = here.shape[1] // 2
    up = shift(here, "y", 4, -1)
    down = shift(here, "y", 4, 1)
    across = jnp.concatenate(
        [shift(down[:, :half], "y", 4, 1), shift(up[:, half:], "y", 4, -1)], axis=1
    )
    mine = jnp.stack([here, up, across, down], axis=1)
    return jnp.concatenate([mine, shift(mine, "core", 2, 1)], axis=2)


def swap_halves(arrays, which):
    half = arrays[0].shape[0] // 2
    keep = [lax.dynamic_slice_in_dim(array, which * half, half, 0) for array in arrays]
    give = [lax.dynamic_slice_in_dim(array, (1 - which) * half, half, 0) for array in arrays]
    got = shift(jnp.concatenate(give, axis=0), "xl", 2, 1)
    return jnp.concatenate(keep, axis=0), got


def gather_z(block):
    half = block.shape[1] // 2
    right, left = [block], [block]
    for _ in range(3):
        right.append(shift(right[-1], "z", 8, 1))
        left.append(shift(left[-1], "z", 8, -1))
    far = jnp.concatenate(
        [shift(right[3][:, :half], "z", 8, 1), shift(left[3][:, half:], "z", 8, -1)], axis=1
    )
    return [block, left[1], left[2], left[3], far, right[3], right[2], right[1]]


def shards(inputs, grad_output, gate_pre, up_pre, gate_weight, up_weight, down_weight):
    xh, y, core = lax.axis_index("xh"), lax.axis_index("y"), lax.axis_index("core")
    z, xl = lax.axis_index("z"), lax.axis_index("xl")
    is_first = xl == 0
    tokens = inputs.shape[0] * 16
    factor = 1.0 / math.sqrt(tokens)

    def rows_at(rows, j):
        start = ((j // 4 - xh) % 2, (j % 4 - y) % 4, 0, 0)
        return lax.dynamic_slice(rows, start, (1, 1) + rows.shape[2:]).reshape(rows.shape[2:])

    near_rows = gather_x(grad_output, is_first)
    down_weight, gate_pre, up_pre = after((down_weight, gate_pre, up_pre), near_rows)
    output_rows = gather_y(near_rows)
    down_units = jnp.concatenate(swap_halves([down_weight], xl), axis=1)

    keep, got = swap_halves([gate_pre.T, up_pre.T], xl)
    saved = jnp.where(
        xl == core,
        jnp.concatenate([keep, got], axis=1),
        jnp.concatenate([got, keep], axis=1),
    )
    units = saved.shape[0] // 2
    gate_value = saved[:units].astype(F32)
    up_value = saved[units:].astype(F32)
    sigmoid_gate = jax.nn.sigmoid(gate_value)
    silu_gate = gate_value * sigmoid_gate
    hidden = (silu_gate * up_value).astype(BF16)
    hidden_blocks = lax.all_gather(hidden, "z", axis=0, tiled=False)

    def ring_sum(weight):
        def part(by):
            return dot(weight, rows_at(output_rows, (z + by) % 8), 1, 1)

        far = part(4)
        right = shift(far[:, :128], "z", 8, 1)
        left = shift(far[:, 128:], "z", 8, -1)
        first = right
        three, back = part(3), part(-3)
        right = shift(jnp.concatenate([three[:, :128] + right, three[:, 128:]], axis=1), "z", 8, 1)
        left = shift(jnp.concatenate([back[:, :128], back[:, 128:] + left], axis=1), "z", 8, -1)
        second = right
        for by in (2, 1):
            right = shift(part(by) + right, "z", 8, 1)
            left = shift(part(-by) + left, "z", 8, -1)
        return part(0) + right + left, first, second

    low, first, second = ring_sum(down_units[: units // 2])
    high, _, _ = ring_sum(down_units[units // 2 :])
    grad_hidden = jnp.concatenate([low, high], axis=0)

    grad_gate_pre = (
        grad_hidden * up_value * sigmoid_gate * (1.0 + gate_value * (1.0 - sigmoid_gate))
    ).astype(BF16)
    grad_up_pre = (grad_hidden * silu_gate).astype(BF16)
    both_blocks = gather_z(jnp.concatenate([grad_gate_pre, grad_up_pre], axis=0))

    inputs = after(inputs, first)
    wide = jnp.concatenate([inputs, shift(inputs, "xl", 2, 1)], axis=1)
    wide = jnp.concatenate([wide, shift(wide, "core", 2, 1)], axis=0)
    input_rows = lax.all_gather(wide, ("xh", "y"), axis=0, tiled=False)
    gate_weight, up_weight = after((gate_weight, up_weight), second)
    both_units = jnp.concatenate(swap_halves([gate_weight, up_weight], xl), axis=1)

    def settle(grad):
        mid = grad.shape[1] // 2
        keep, got = grad[:, :mid], shift(grad[:, mid:], "xl", 2, 1)

        def ordered(start):
            rows = slice(start, start + units)
            return jnp.where(
                is_first,
                jnp.concatenate([keep[rows], got[rows]], axis=0),
                jnp.concatenate([got[rows], keep[rows]], axis=0),
            )

        return [ordered(start) for start in range(0, grad.shape[0], units)]

    total = None
    for j in range(8):
        term = dot(hidden_blocks[j], rows_at(output_rows, j), 1, 0)
        total = term if total is None else total + term
    (grad_down,) = settle(total * factor)

    partial_input = jnp.stack([dot(block, both_units, 0, 0) for block in both_blocks])
    lanes = partial_input.shape[2] // 2

    def sent(value, axis, size, by):
        return shift(value.astype(BF16), axis, size, by).astype(F32)

    summed = partial_input[:, :128] + sent(partial_input[:, 128:], "core", 2, 1)

    def toward(xr, yr):
        j = ((xh + xr) % 2) * 4 + (y + yr) % 4
        return lax.dynamic_slice_in_dim(summed, (j - z) % 8, 1, 0)

    def toward_y(yr):
        return jnp.concatenate([toward(0, yr), toward(1, yr)], axis=0)

    across = toward_y(2)
    a, b = sent(across[:, :64], "y", 4, 1), sent(across[:, 64:], "y", 4, -1)
    one, three = toward_y(1), toward_y(3)
    one = jnp.concatenate([one[:, :64] + a, one[:, 64:]], axis=1)
    three = jnp.concatenate([three[:, :64], three[:, 64:] + b], axis=1)
    summed_y = toward_y(0) + sent(one, "y", 4, 1) + sent(three, "y", 4, -1)

    ring = ("xh", "xl")
    near, beyond = summed_y[0, :, lanes:], summed_y[1, :, lanes:]
    opposite = summed_y[1, :, :lanes]
    a, b = sent(opposite[:64], ring, 4, 1), sent(opposite[64:], ring, 4, -1)
    one = jnp.where(is_first, near, beyond)
    three = jnp.where(is_first, beyond, near)
    one = jnp.concatenate([one[:64] + a, one[64:]], axis=0)
    three = jnp.concatenate([three[:64], three[64:] + b], axis=0)
    grad_input = summed_y[0, :, :lanes] + sent(one, ring, 4, 1) + sent(three, ring, 4, -1)

    total = None
    for by in (0, 1, 7, 2, 6, 3, 5, 4):
        rows = lax.dynamic_index_in_dim(input_rows, (z + by) % 8, 0, keepdims=False)
        term = dot(both_blocks[by], rows, 1, 0)
        total = term if total is None else total + term
    grad_gate, grad_up = settle(total * factor)
    return grad_input, grad_gate, grad_up, grad_down


def solution(mesh):
    fine = Mesh(mesh.devices.reshape(2, 4, 2, 8, 2), ("xh", "y", "core", "z", "xl"))
    rows_cols = P(("xh", "y", "core"), ("z", "xl"))
    cols_rows = P(("z", "xl"), ("xh", "y", "core"))
    return jax.shard_map(
        shards,
        mesh=fine,
        in_specs=(rows_cols, rows_cols, cols_rows, cols_rows, rows_cols, rows_cols, rows_cols),
        out_specs=(rows_cols,) * 4,
        check_vma=False,
    )
```

```python
import math

import jax
import jax.numpy as jnp
from jax import lax
from jax.sharding import Mesh, PartitionSpec as P

F32 = jnp.float32
BF16 = jnp.bfloat16


def shift(value, axis, size, by):
    return lax.ppermute(value, axis, [(i, (i + by) % size) for i in range(size)])


def dot(left, right, left_dim, right_dim):
    return lax.dot_general(
        left, right, (((left_dim,), (right_dim,)), ((), ())), preferred_element_type=F32
    )


def after(value, *others):
    return lax.optimization_barrier((value,) + others)[0]


def gather_x(block, is_first):
    ring = ("xh", "xl")
    half = block.shape[0] // 2
    from_right = shift(block, ring, 4, -1)
    from_left = shift(block, ring, 4, 1)
    far = jnp.concatenate(
        [shift(from_left[:half], ring, 4, 1), shift(from_right[half:], ring, 4, -1)], axis=0
    )
    same = jnp.where(is_first, from_right, from_left)
    other = jnp.where(is_first, from_left, from_right)
    rows = jnp.stack(
        [jnp.concatenate([block, same], axis=1), jnp.concatenate([far, other], axis=1)]
    )
    return rows, from_right


def gather_y(here):
    half = here.shape[1] // 2
    up = shift(here, "y", 4, -1)
    down = shift(here, "y", 4, 1)
    across = jnp.concatenate(
        [shift(down[:, :half], "y", 4, 1), shift(up[:, half:], "y", 4, -1)], axis=1
    )
    mine = jnp.stack([here, up, across, down], axis=1)
    return jnp.concatenate([mine, shift(mine, "core", 2, 1)], axis=2)


def swap_halves(arrays, which):
    half = arrays[0].shape[0] // 2
    keep = [lax.dynamic_slice_in_dim(array, which * half, half, 0) for array in arrays]
    give = [lax.dynamic_slice_in_dim(array, (1 - which) * half, half, 0) for array in arrays]
    got = shift(jnp.concatenate(give, axis=0), "xl", 2, 1)
    return jnp.concatenate(keep, axis=0), got


def shards(inputs, grad_output, gate_pre, up_pre, gate_weight, up_weight, down_weight):
    xh, y, core = lax.axis_index("xh"), lax.axis_index("y"), lax.axis_index("core")
    z, xl = lax.axis_index("z"), lax.axis_index("xl")
    is_first = xl == 0
    tokens = inputs.shape[0] * 16
    factor = 1.0 / math.sqrt(tokens)

    def rows_at(rows, j):
        start = ((j // 4 - xh) % 2, (j % 4 - y) % 4, 0, 0)
        return lax.dynamic_slice(rows, start, (1, 1) + rows.shape[2:]).reshape(rows.shape[2:])

    near_rows, hop = gather_x(grad_output, is_first)
    gate_pre, up_pre = after((gate_pre, up_pre), hop)
    down_weight = after(down_weight, near_rows)
    output_rows = gather_y(near_rows)
    down_units = jnp.concatenate(swap_halves([down_weight], xl), axis=1)

    keep, got = swap_halves([gate_pre.T, up_pre.T], xl)
    saved = jnp.where(
        xl == core,
        jnp.concatenate([keep, got], axis=1),
        jnp.concatenate([got, keep], axis=1),
    )
    units = saved.shape[0] // 2
    gate_value = saved[:units].astype(F32)
    up_value = saved[units:].astype(F32)
    sigmoid_gate = jax.nn.sigmoid(gate_value)
    silu_gate = gate_value * sigmoid_gate
    hidden = (silu_gate * up_value).astype(BF16)
    hidden_blocks = lax.all_gather(hidden, "z", axis=0, tiled=False)

    inputs = after(inputs, near_rows)
    wide = jnp.concatenate([inputs, shift(inputs, "xl", 2, 1)], axis=1)
    wide = jnp.concatenate([wide, shift(wide, "core", 2, 1)], axis=0)
    input_rows = lax.all_gather(after(wide, hidden_blocks), ("xh", "y"), axis=0, tiled=False)

    def ring_sum(weight, gathered=None):
        def part(by):
            return dot(weight, rows_at(output_rows, (z + by) % 8), 1, 1)

        far = part(4)
        right = shift(far[:, :128], "z", 8, 1)
        left = shift(far[:, 128:], "z", 8, -1)
        first = right
        three, back = part(3), part(-3)
        right = shift(jnp.concatenate([three[:, :128] + right, three[:, 128:]], axis=1), "z", 8, 1)
        left = shift(jnp.concatenate([back[:, :128], back[:, 128:] + left], axis=1), "z", 8, -1)
        second = right
        for by in (2, 1):
            if by == 1 and gathered is not None:
                right = after(right, gathered)
            right = shift(part(by) + right, "z", 8, 1)
            left = shift(part(-by) + left, "z", 8, -1)
        return part(0) + right + left, first, second

    low, first, second = ring_sum(down_units[: units // 2], hidden_blocks)
    high, _, _ = ring_sum(down_units[units // 2 :])
    grad_hidden = jnp.concatenate([low, high], axis=0)

    grad_gate_pre = (
        grad_hidden * up_value * sigmoid_gate * (1.0 + gate_value * (1.0 - sigmoid_gate))
    ).astype(BF16)
    grad_up_pre = (grad_hidden * silu_gate).astype(BF16)
    gate_weight, up_weight = after((gate_weight, up_weight), second)
    both_units = jnp.concatenate(swap_halves([gate_weight, up_weight], xl), axis=1)

    both = jnp.concatenate([grad_gate_pre, grad_up_pre], axis=0)
    right, left = [both], [both]
    for _ in range(3):
        right.append(shift(right[-1], "z", 8, 1))
        left.append(shift(left[-1], "z", 8, -1))
    far = (shift(right[3][:, :128], "z", 8, 1), shift(left[3][:, 128:], "z", 8, -1))

    def kept_and_sent(blocks):
        kept = [dot(block[:, :128], both_units, 0, 0) for block in blocks]
        out = [dot(block[:, 128:], both_units, 0, 0).astype(BF16) for block in blocks]
        return jnp.stack(kept), jnp.stack(out)

    def core_sum(kept, out):
        return kept + shift(out, "core", 2, 1).astype(F32)

    early = core_sum(*kept_and_sent([both, left[1], right[1], left[2], right[2]]))
    late = kept_and_sent([left[3], right[3]])
    far, early, late, input_rows = after((far, early, late, input_rows))
    far = jnp.concatenate(far, axis=1)
    last = kept_and_sent([far])
    late = core_sum(*(jnp.concatenate(pair, axis=0) for pair in zip(late, last)))
    order = (early[0], early[1], early[3], late[0], late[2], late[1], early[4], early[2])
    both_blocks = [both, left[1], left[2], left[3], far, right[3], right[2], right[1]]
    summed = jnp.stack(order)
    lanes = summed.shape[2] // 2

    def settle(grad):
        mid = grad.shape[1] // 2
        keep, got = grad[:, :mid], shift(grad[:, mid:], "xl", 2, 1)

        def ordered(start):
            rows = slice(start, start + units)
            return jnp.where(
                is_first,
                jnp.concatenate([keep[rows], got[rows]], axis=0),
                jnp.concatenate([got[rows], keep[rows]], axis=0),
            )

        return [ordered(start) for start in range(0, grad.shape[0], units)]

    total = None
    for j in range(8):
        term = dot(hidden_blocks[j], rows_at(output_rows, j), 1, 0)
        total = term if total is None else total + term
    (grad_down,) = settle(total * factor)

    def sent(value, axis, size, by):
        return shift(value.astype(BF16), axis, size, by).astype(F32)

    def toward(xr, yr):
        j = ((xh + xr) % 2) * 4 + (y + yr) % 4
        return lax.dynamic_slice_in_dim(summed, (j - z) % 8, 1, 0)

    def toward_y(yr):
        return jnp.concatenate([toward(0, yr), toward(1, yr)], axis=0)

    across = toward_y(2)
    a, b = sent(across[:, :64], "y", 4, 1), sent(across[:, 64:], "y", 4, -1)
    one, three = toward_y(1), toward_y(3)
    one = jnp.concatenate([one[:, :64] + a, one[:, 64:]], axis=1)
    three = jnp.concatenate([three[:, :64], three[:, 64:] + b], axis=1)
    summed_y = toward_y(0) + sent(one, "y", 4, 1) + sent(three, "y", 4, -1)

    ring = ("xh", "xl")
    near, beyond = summed_y[0, :, lanes:], summed_y[1, :, lanes:]
    opposite = summed_y[1, :, :lanes]
    a, b = sent(opposite[:64], ring, 4, 1), sent(opposite[64:], ring, 4, -1)
    one = jnp.where(is_first, near, beyond)
    three = jnp.where(is_first, beyond, near)
    one = jnp.concatenate([one[:64] + a, one[64:]], axis=0)
    three = jnp.concatenate([three[:64], three[64:] + b], axis=0)
    grad_input = summed_y[0, :, :lanes] + sent(one, ring, 4, 1) + sent(three, ring, 4, -1)

    total = None
    for by in (0, 1, 7, 2, 6, 3, 5, 4):
        rows = lax.dynamic_index_in_dim(input_rows, (z + by) % 8, 0, keepdims=False)
        term = dot(both_blocks[by], rows, 1, 0)
        total = term if total is None else total + term
    grad_gate, grad_up = settle(total * factor)
    return grad_input, grad_gate, grad_up, grad_down


def solution(mesh):
    fine = Mesh(mesh.devices.reshape(2, 4, 2, 8, 2), ("xh", "y", "core", "z", "xl"))
    rows_cols = P(("xh", "y", "core"), ("z", "xl"))
    cols_rows = P(("z", "xl"), ("xh", "y", "core"))
    return jax.shard_map(
        shards,
        mesh=fine,
        in_specs=(rows_cols, rows_cols, cols_rows, cols_rows, rows_cols, rows_cols, rows_cols),
        out_specs=(rows_cols,) * 4,
        check_vma=False,
    )
```

```python
import math

import jax
import jax.numpy as jnp
from jax import lax
from jax.sharding import Mesh, PartitionSpec as P

F32 = jnp.float32
BF16 = jnp.bfloat16


def shift(value, axis, size, by):
    return lax.ppermute(value, axis, [(i, (i + by) % size) for i in range(size)])


def sent(value, axis, size, by):
    return shift(value.astype(BF16), axis, size, by).astype(F32)


def dot(left, right, left_dim, right_dim):
    return lax.dot_general(
        left, right, (((left_dim,), (right_dim,)), ((), ())), preferred_element_type=F32
    )


def after(value, *others):
    return lax.optimization_barrier((value,) + others)[0]


def gather_x(block, is_first):
    ring = ("xh", "xl")
    from_right = shift(block, ring, 4, -1)
    from_left = shift(block, ring, 4, 1)
    far = shift(block, ring, 4, 2)
    same = jnp.where(is_first, from_right, from_left)
    other = jnp.where(is_first, from_left, from_right)
    return jnp.stack(
        [jnp.concatenate([block, same], axis=1), jnp.concatenate([far, other], axis=1)]
    )


def gather_y(here):
    up = shift(here, "y", 4, -1)
    down = shift(here, "y", 4, 1)
    return jnp.stack([here, up, shift(here, "y", 4, 2), down], axis=1)


def swap_halves(arrays, which):
    half = arrays[0].shape[0] // 2
    keep = [lax.dynamic_slice_in_dim(array, which * half, half, 0) for array in arrays]
    give = [lax.dynamic_slice_in_dim(array, (1 - which) * half, half, 0) for array in arrays]
    got = shift(jnp.concatenate(give, axis=0), "xl", 2, 1)
    return jnp.concatenate(keep, axis=0), got


def shards(inputs, grad_output, gate_pre, up_pre, gate_weight, up_weight, down_weight):
    xh, y, core = lax.axis_index("xh"), lax.axis_index("y"), lax.axis_index("core")
    z, xl = lax.axis_index("z"), lax.axis_index("xl")
    is_first = xl == 0
    block = inputs.shape[0]
    factor = 1.0 / math.sqrt(block * 16)

    def rows_at(rows, j):
        start = ((j // 4 - xh) % 2, (j % 4 - y) % 4, 0, 0)
        return lax.dynamic_slice(rows, start, (1, 1) + rows.shape[2:]).reshape(rows.shape[2:])

    gate_here, up_here = gate_pre.astype(F32), up_pre.astype(F32)
    hidden = (gate_here * jax.nn.sigmoid(gate_here) * up_here).astype(BF16)
    hidden_rows = lax.all_gather(hidden, "z", axis=0, tiled=True)

    near_rows = gather_x(grad_output, is_first)
    down_weight = after(down_weight, near_rows)
    down_units = after(jnp.concatenate(swap_halves([down_weight], xl), axis=1))
    own_rows = gather_y(near_rows)
    core_rows = shift(own_rows, "core", 2, 1)
    output_rows = jnp.concatenate([own_rows, core_rows], axis=2)

    def ring_sum(weight, gathered=None):
        def part(by):
            return dot(weight, rows_at(output_rows, (z + by) % 8), 1, 1)

        opposite = (z + 4) % 8
        right = shift(dot(weight, rows_at(own_rows, opposite), 1, 1), "z", 8, 1)
        left = shift(dot(weight, rows_at(core_rows, opposite), 1, 1), "z", 8, -1)
        hops = [right]
        three, back = part(3), part(-3)
        right = shift(
            jnp.concatenate([three[:, :block] + right, three[:, block:]], axis=1), "z", 8, 1
        )
        left = shift(
            jnp.concatenate([back[:, :block], back[:, block:] + left], axis=1), "z", 8, -1
        )
        hops.append(right)
        for by in (2, 1):
            if by == 1 and gathered is not None:
                right = after(right, gathered)
            right = shift(part(by) + right, "z", 8, 1)
            left = shift(part(-by) + left, "z", 8, -1)
            hops.append(right)
        return part(0) + right + left, hops

    half = down_units.shape[0] // 2
    low, hops = ring_sum(down_units[:half], hidden_rows)
    high, _ = ring_sum(down_units[half:])
    grad_hidden = jnp.concatenate([low, high], axis=0)

    inputs = after(inputs, hops[0])
    wide = jnp.concatenate([inputs, shift(inputs, "xl", 2, 1)], axis=1)
    wide = jnp.concatenate([wide, shift(wide, "core", 2, 1)], axis=0)
    input_rows = lax.all_gather(wide, ("xh", "y"), axis=0, tiled=False)

    gate_pre, up_pre = after((gate_pre, up_pre), hops[0])
    keep, got = swap_halves([gate_pre.T, up_pre.T], xl)
    saved = jnp.where(
        xl == core,
        jnp.concatenate([keep, got], axis=1),
        jnp.concatenate([got, keep], axis=1),
    )
    units = saved.shape[0] // 2
    gate_value = saved[:units].astype(F32)
    up_value = saved[units:].astype(F32)
    sigmoid_gate = jax.nn.sigmoid(gate_value)
    to_gate = up_value * sigmoid_gate * (1.0 + gate_value * (1.0 - sigmoid_gate))
    slopes = after(jnp.concatenate([to_gate, gate_value * sigmoid_gate], axis=0))

    gate_weight, up_weight = after((gate_weight, up_weight), hops[1])
    both_units = after(jnp.concatenate(swap_halves([gate_weight, up_weight], xl), axis=1))

    both = (jnp.concatenate([grad_hidden, grad_hidden], axis=0) * slopes).astype(BF16)
    right, left = [both], [both]
    for _ in range(3):
        right.append(shift(right[-1], "z", 8, 1))
        left.append(shift(left[-1], "z", 8, -1))
    far = (shift(right[3][:, :block], "z", 8, 1), shift(left[3][:, block:], "z", 8, -1))

    start = jnp.where(xl == core, 0, block)
    own_tokens = jnp.concatenate(
        [lax.dynamic_slice_in_dim(rows_at(output_rows, j), start, block, 0) for j in range(8)],
        axis=0,
    )
    partial_down = dot(hidden_rows, own_tokens, 0, 0)
    lanes = partial_down.shape[1] // 2
    grad_down = (partial_down[:, :lanes] + shift(partial_down[:, lanes:], "xl", 2, 1)) * factor

    def kept_and_sent(pairs):
        kept = [dot(pair[0], both_units, 0, 0) for pair in pairs]
        out = [dot(pair[1], both_units, 0, 0).astype(BF16) for pair in pairs]
        return jnp.stack(kept), jnp.stack(out)

    def core_sum(kept, out):
        return kept + shift(out, "core", 2, 1).astype(F32)

    def halves(value):
        return value[:, :block], value[:, block:]

    near = [both, left[1], right[1], left[2], right[2]]
    early = core_sum(*kept_and_sent([halves(value) for value in near]))
    late = kept_and_sent([halves(left[3]), halves(right[3])])
    far, early, late, input_rows = after((far, early, late, input_rows))
    last = kept_and_sent([far])
    late = core_sum(*(jnp.concatenate(pair, axis=0) for pair in zip(late, last)))
    summed = jnp.concatenate([early, late], axis=0)

    def input_at(by):
        return lax.dynamic_index_in_dim(input_rows, (z + by) % 8, 0, keepdims=False)

    near += [left[3], right[3]]
    total = sum(dot(value, input_at(by), 1, 0) for value, by in zip(near, (0, 1, 7, 2, 6, 3, 5)))
    opposite = input_at(4)
    total = total + dot(far[0], opposite[:block], 1, 0) + dot(far[1], opposite[block:], 1, 0)
    total = total * factor
    summed, total = after((summed, total))

    def toward(xr, yr):
        by = (((xh + xr) % 2) * 4 + (y + yr) % 4 - z) % 8
        slot = jnp.maximum(0, 2 * jnp.minimum(by, 8 - by) - 1 + (by > 4))
        return lax.dynamic_slice_in_dim(summed, slot, 1, 0)

    def toward_y(yr):
        return jnp.concatenate([toward(0, yr), toward(1, yr)], axis=0)

    summed = (
        toward_y(0)
        + sent(toward_y(1), "y", 4, 1)
        + sent(toward_y(3), "y", 4, -1)
        + sent(toward_y(2), "y", 4, 2)
    )
    ring = ("xh", "xl")
    side, beyond = summed[0, :, lanes:], summed[1, :, lanes:]
    grad_input = (
        summed[0, :, :lanes]
        + sent(jnp.where(is_first, side, beyond), ring, 4, 1)
        + sent(jnp.where(is_first, beyond, side), ring, 4, -1)
        + sent(summed[1, :, :lanes], ring, 4, 2)
    )

    keep, got = total[:, :lanes], shift(total[:, lanes:], "xl", 2, 1)

    def ordered(rows):
        return jnp.where(
            is_first,
            jnp.concatenate([keep[rows], got[rows]], axis=0),
            jnp.concatenate([got[rows], keep[rows]], axis=0),
        )

    grad_gate, grad_up = ordered(slice(0, units)), ordered(slice(units, 2 * units))
    return grad_input, grad_gate, grad_up, grad_down


def solution(mesh):
    fine = Mesh(mesh.devices.reshape(2, 4, 2, 8, 2), ("xh", "y", "core", "z", "xl"))
    rows_cols = P(("xh", "y", "core"), ("z", "xl"))
    cols_rows = P(("z", "xl"), ("xh", "y", "core"))
    return jax.shard_map(
        shards,
        mesh=fine,
        in_specs=(rows_cols, rows_cols, cols_rows, cols_rows, rows_cols, rows_cols, rows_cols),
        out_specs=(rows_cols,) * 4,
        check_vma=False,
    )
```

```python
import math

import jax
import jax.numpy as jnp
from jax import lax
from jax.sharding import Mesh, PartitionSpec as P

F32 = jnp.float32
BF16 = jnp.bfloat16
X = ("xh", "xl")


def shift(value, axis, size, by):
    return lax.ppermute(value, axis, [(i, (i + by) % size) for i in range(size)])


def sent(value, axis, size, by):
    return shift(value.astype(BF16), axis, size, by).astype(F32)


def dot(left, right, left_dim, right_dim):
    return lax.dot_general(
        left, right, (((left_dim,), (right_dim,)), ((), ())), preferred_element_type=F32
    )


def after(value, *others):
    return lax.optimization_barrier((value,) + others)[0]


def gather_x(block, is_first, *others):
    from_right = shift(block, X, 4, -1)
    from_left = shift(block, X, 4, 1)
    far = shift(block, X, 4, 2)
    from_right, from_left = after((from_right, from_left), *others)
    same = jnp.where(is_first, from_right, from_left)
    other = jnp.where(is_first, from_left, from_right)
    return jnp.stack(
        [jnp.concatenate([block, same], axis=1), jnp.concatenate([far, other], axis=1)]
    )


def shards(inputs, grad_output, gate_pre, up_pre, gate_weight, up_weight, down_weight):
    xh, y, core = lax.axis_index("xh"), lax.axis_index("y"), lax.axis_index("core")
    z, xl = lax.axis_index("z"), lax.axis_index("xl")
    is_first = xl == 0
    block = inputs.shape[0]
    units = gate_weight.shape[0] // 2
    factor = 1.0 / math.sqrt(block * 16)

    def place(by):
        j = (z + by) % 8
        return ((j // 4 - xh) % 2, (j % 4 - y) % 4)

    def rows_at(rows, by):
        return lax.dynamic_slice(
            rows, place(by) + (0, 0), (1, 1) + rows.shape[2:]
        ).reshape(rows.shape[2:])

    gate_here, up_here = gate_pre.astype(F32), up_pre.astype(F32)
    hidden = (gate_here * jax.nn.sigmoid(gate_here) * up_here).astype(BF16)
    near = gather_x(grad_output, is_first, hidden)
    hidden_blocks = lax.all_gather(hidden, "z", axis=0, tiled=False)

    def half(array, which):
        return lax.dynamic_slice_in_dim(array, which * units, units, 0)

    theirs_down = shift(half(after(down_weight, near), 1 - xl), "xl", 2, 1)
    up = shift(near, "y", 4, -1)
    down = shift(near, "y", 4, 1)
    across = shift(near, "y", 4, 2)
    inputs, gate_pre, up_pre, gate_weight, up_weight = after(
        (inputs, gate_pre, up_pre, gate_weight, up_weight), up
    )
    turned = (gate_pre.T, up_pre.T)

    def side(which):
        saved = jnp.concatenate([half(array, which) for array in turned], axis=1)
        return jnp.concatenate([saved, half(gate_weight, which), half(up_weight, which)], axis=0)

    wide = jnp.concatenate([inputs, shift(inputs, "xl", 2, 1)], axis=1)
    wide = jnp.concatenate([wide, shift(wide, "core", 2, 1)], axis=0)
    give, mine, wide, across = after((side(1 - xl), side(xl), wide, across))
    input_rows = lax.all_gather(wide, ("xh", "y"), axis=0, tiled=False)
    own_rows = jnp.stack([near, up, across, down], axis=1)
    core_rows = shift(own_rows, "core", 2, 1)
    output_rows = jnp.concatenate([own_rows, core_rows], axis=2)

    down_units = after(jnp.concatenate([half(down_weight, xl), theirs_down], axis=1))
    weights = (down_units[: units // 2], down_units[units // 2 :])

    def parts(by):
        rows = rows_at(output_rows, by)
        return [dot(weight, rows, 1, 1) for weight in weights]

    right = [dot(weight, rows_at(own_rows, 4), 1, 1) for weight in weights]
    left = [dot(weight, rows_at(core_rows, 4), 1, 1) for weight in weights]
    right, left = lax.optimization_barrier((right, left))
    theirs = shift(after(give, right, left), "xl", 2, 1)
    right = [shift(value, "z", 8, 1) for value in right]
    left = [shift(value, "z", 8, -1) for value in left]
    right = [
        jnp.concatenate([part[:, :block] + value, part[:, block:]], axis=1)
        for part, value in zip(parts(3), right)
    ]
    left = [
        jnp.concatenate([part[:, :block], part[:, block:] + value], axis=1)
        for part, value in zip(parts(-3), left)
    ]
    mine, theirs = [
        [side[i * units : (i + 1) * units] for i in range(3)] for side in (mine, theirs)
    ]
    for by in (2, 1):
        right = [shift(value, "z", 8, 1) for value in right]
        left = [shift(value, "z", 8, -1) for value in left]
        right = [part + value for part, value in zip(parts(by), right)]
        left = [part + value for part, value in zip(parts(-by), left)]
    right = [shift(value, "z", 8, 1) for value in right]
    left = [shift(value, "z", 8, -1) for value in left]
    gates = [
        jnp.where(
            xl == core,
            jnp.concatenate([a, b], axis=1),
            jnp.concatenate([b, a], axis=1),
        ).astype(F32)
        for a, b in (
            (mine[0][:, :block], theirs[0][:, :block]),
            (mine[0][:, block:], theirs[0][:, block:]),
        )
    ]
    gate_value, up_value = gates
    sigmoid_gate = jax.nn.sigmoid(gate_value)
    to_gate = up_value * sigmoid_gate * (1.0 + gate_value * (1.0 - sigmoid_gate))
    slopes = after(jnp.concatenate([to_gate, gate_value * sigmoid_gate], axis=0))
    both_units = after(
        jnp.concatenate(
            [jnp.concatenate([a, b], axis=1) for a, b in zip(mine[1:], theirs[1:])], axis=0
        )
    )

    right, left = after((right, left), slopes, both_units)
    grad_hidden = jnp.concatenate(
        [part + a + b for part, a, b in zip(parts(0), right, left)], axis=0
    )

    both = (jnp.concatenate([grad_hidden, grad_hidden], axis=0) * slopes).astype(BF16)
    start = jnp.where(xl == core, 0, block)
    size = (1, 1, block, output_rows.shape[3])
    lanes = size[3] // 2

    def kept_and_sent(pairs):
        kept = [dot(pair[0], both_units, 0, 0) for pair in pairs]
        out = [dot(pair[1], both_units, 0, 0).astype(BF16) for pair in pairs]
        return jnp.stack(kept), jnp.stack(out)

    def core_sum(kept, out):
        return kept + shift(out, "core", 2, 1).astype(F32)

    def halves(value):
        return value[:, :block], value[:, block:]

    def input_at(by):
        return lax.dynamic_index_in_dim(input_rows, (z + by) % 8, 0, keepdims=False)

    def weights_of(values, by, total=None):
        for value, k in zip(values, by):
            term = dot(value, input_at(k), 1, 0)
            total = after(term if total is None else total + term)
        return total

    def next_pair(pair, *others):
        return after((shift(pair[0], "z", 8, 1), shift(pair[1], "z", 8, -1)), *others)

    partial_down = None
    for j, value in enumerate(hidden_blocks):
        rows = lax.dynamic_slice(output_rows, place(j - z) + (start, 0), size).reshape(size[2:])
        term = dot(value, rows, 0, 0)
        partial_down = after(term if partial_down is None else partial_down + term)
    keep_down, give_down = partial_down[:, :lanes], partial_down[:, lanes:].astype(BF16)

    one = next_pair((both, both), keep_down, give_down)
    first = kept_and_sent([halves(value) for value in (both, one[1], one[0])])
    total = weights_of((both,), (0,))
    two = next_pair(one, first)
    first = core_sum(*first)
    second = kept_and_sent([halves(value) for value in (two[1], two[0])])
    total = weights_of((one[1], one[0]), (1, 7), total)
    grad_down = (keep_down + shift(give_down, "xl", 2, 1).astype(F32)) * factor
    three = next_pair(two, second, total, grad_down)
    third = kept_and_sent([halves(value) for value in (three[1], three[0])])
    late = tuple(jnp.concatenate(pair, axis=0) for pair in zip(second, third))
    total = weights_of((two[1], two[0], three[1], three[0]), (2, 6, 3, 5), total)
    far = (shift(three[0][:, :block], "z", 8, 1), shift(three[1][:, block:], "z", 8, -1))
    early = first
    far, early, late, total = after((far, early, late, total))
    last = kept_and_sent([far])
    late = core_sum(*(jnp.concatenate(pair, axis=0) for pair in zip(late, last)))
    summed = jnp.concatenate([early, late], axis=0)
    total = (total + dot(jnp.concatenate(far, axis=1), input_at(4), 1, 0)) * factor
    keep, give = total[:, :lanes], total[:, lanes:].astype(BF16)
    summed, give = after((summed, give))
    got = shift(give, "xl", 2, 1).astype(F32)

    def toward(xr, yr):
        by = (((xh + xr) % 2) * 4 + (y + yr) % 4 - z) % 8
        slot = jnp.maximum(0, 2 * jnp.minimum(by, 8 - by) - 1 + (by > 4))
        return lax.dynamic_slice_in_dim(summed, slot, 1, 0)

    def toward_y(yr):
        return jnp.concatenate([toward(0, yr), toward(1, yr)], axis=0)

    summed = (
        toward_y(0)
        + sent(toward_y(1), "y", 4, 1)
        + sent(toward_y(3), "y", 4, -1)
        + sent(toward_y(2), "y", 4, 2)
    )
    level, beyond = summed[0, :, lanes:], summed[1, :, lanes:]
    arrived = (
        sent(jnp.where(is_first, level, beyond), X, 4, 1),
        sent(jnp.where(is_first, beyond, level), X, 4, -1),
        sent(summed[1, :, :lanes], X, 4, 2),
    )

    def ordered(rows):
        return jnp.where(
            is_first,
            jnp.concatenate([keep[rows], got[rows]], axis=0),
            jnp.concatenate([got[rows], keep[rows]], axis=0),
        )

    grad_gate, grad_up = ordered(slice(0, units)), ordered(slice(units, 2 * units))
    arrived, grad_gate, grad_up = after((arrived, grad_gate, grad_up))
    grad_input = summed[0, :, :lanes] + sum(arrived)
    return grad_input, grad_gate, grad_up, grad_down


def solution(mesh):
    fine = Mesh(mesh.devices.reshape(2, 4, 2, 8, 2), ("xh", "y", "core", "z", "xl"))
    rows_cols = P(("xh", "y", "core"), ("z", "xl"))
    cols_rows = P(("z", "xl"), ("xh", "y", "core"))
    return jax.shard_map(
        shards,
        mesh=fine,
        in_specs=(rows_cols, rows_cols, cols_rows, cols_rows, rows_cols, rows_cols, rows_cols),
        out_specs=(rows_cols,) * 4,
        check_vma=False,
    )
```

```python
import math

import jax
import jax.numpy as jnp
from jax import lax
from jax.sharding import Mesh, PartitionSpec as P

F32 = jnp.float32
BF16 = jnp.bfloat16
X = ("xh", "xl")


def shift(value, axis, size, by):
    return lax.ppermute(value, axis, [(i, (i + by) % size) for i in range(size)])


def sent(value, axis, size, by):
    return shift(value.astype(BF16), axis, size, by).astype(F32)


def dot(left, right, left_dim, right_dim):
    return lax.dot_general(
        left, right, (((left_dim,), (right_dim,)), ((), ())), preferred_element_type=F32
    )


def after(value, *others):
    return lax.optimization_barrier((value,) + others)[0]


def gather_x(block, is_first, *others):
    from_right = shift(block, X, 4, -1)
    from_left = shift(block, X, 4, 1)
    far = shift(block, X, 4, 2)
    from_right, from_left = after((from_right, from_left), *others)
    same = jnp.where(is_first, from_right, from_left)
    other = jnp.where(is_first, from_left, from_right)
    return jnp.stack(
        [jnp.concatenate([block, same], axis=1), jnp.concatenate([far, other], axis=1)]
    )


def shards(inputs, grad_output, gate_pre, up_pre, gate_weight, up_weight, down_weight):
    xh, y, core = lax.axis_index("xh"), lax.axis_index("y"), lax.axis_index("core")
    z, xl = lax.axis_index("z"), lax.axis_index("xl")
    is_first = xl == 0
    block = inputs.shape[0]
    units = gate_weight.shape[0] // 2
    factor = 1.0 / math.sqrt(block * 16)

    def place(by):
        j = (z + by) % 8
        return ((j // 4 - xh) % 2, (j % 4 - y) % 4)

    def rows_at(rows, by):
        return lax.dynamic_slice(
            rows, place(by) + (0, 0), (1, 1) + rows.shape[2:]
        ).reshape(rows.shape[2:])

    gate_here, up_here = gate_pre.astype(F32), up_pre.astype(F32)
    hidden = (gate_here * jax.nn.sigmoid(gate_here) * up_here).astype(BF16)
    near = gather_x(grad_output, is_first, hidden)
    hidden_blocks = lax.all_gather(hidden, "z", axis=0, tiled=False)

    def half(array, which):
        return lax.dynamic_slice_in_dim(array, which * units, units, 0)

    theirs_down = shift(half(after(down_weight, near), 1 - xl), "xl", 2, 1)
    up = shift(near, "y", 4, -1)
    down = shift(near, "y", 4, 1)
    across = shift(near, "y", 4, 2)
    inputs, gate_pre, up_pre, gate_weight, up_weight = after(
        (inputs, gate_pre, up_pre, gate_weight, up_weight), up
    )
    turned = (gate_pre.T, up_pre.T)

    def side(which):
        saved = jnp.concatenate([half(array, which) for array in turned], axis=1)
        return jnp.concatenate([saved, half(gate_weight, which), half(up_weight, which)], axis=0)

    wide = jnp.concatenate([inputs, shift(inputs, "xl", 2, 1)], axis=1)
    wide = jnp.concatenate([wide, shift(wide, "core", 2, 1)], axis=0)
    give, mine, wide, across = after((side(1 - xl), side(xl), wide, across))
    input_rows = lax.all_gather(wide, ("xh", "y"), axis=0, tiled=False)
    own_rows = jnp.stack([near, up, across, down], axis=1)
    core_rows = shift(own_rows, "core", 2, 1)
    output_rows = jnp.concatenate([own_rows, core_rows], axis=2)

    down_units = after(jnp.concatenate([half(down_weight, xl), theirs_down], axis=1))
    weights = (down_units[: units // 2], down_units[units // 2 :])

    def parts(by):
        rows = rows_at(output_rows, by)
        return [dot(weight, rows, 1, 1) for weight in weights]

    right = [dot(weight, rows_at(own_rows, 4), 1, 1) for weight in weights]
    left = [dot(weight, rows_at(core_rows, 4), 1, 1) for weight in weights]
    right, left = after(right), after(left)
    theirs = shift(after(give, right, left), "xl", 2, 1)
    right = [shift(value, "z", 8, 1) for value in right]
    left = [shift(value, "z", 8, -1) for value in left]
    right = [
        jnp.concatenate([part[:, :block] + value, part[:, block:]], axis=1)
        for part, value in zip(parts(3), right)
    ]
    left = [
        jnp.concatenate([part[:, :block], part[:, block:] + value], axis=1)
        for part, value in zip(parts(-3), left)
    ]
    mine, theirs = [
        [side[i * units : (i + 1) * units] for i in range(3)] for side in (mine, theirs)
    ]
    for by in (2, 1):
        right = [shift(value, "z", 8, 1) for value in right]
        left = [shift(value, "z", 8, -1) for value in left]
        right = [part + value for part, value in zip(parts(by), right)]
        left = [part + value for part, value in zip(parts(-by), left)]
    right = [shift(value, "z", 8, 1) for value in right]
    left = [shift(value, "z", 8, -1) for value in left]
    gates = [
        jnp.where(
            xl == core,
            jnp.concatenate([a, b], axis=1),
            jnp.concatenate([b, a], axis=1),
        ).astype(F32)
        for a, b in (
            (mine[0][:, :block], theirs[0][:, :block]),
            (mine[0][:, block:], theirs[0][:, block:]),
        )
    ]
    gate_value, up_value = gates
    sigmoid_gate = jax.nn.sigmoid(gate_value)
    to_gate = up_value * sigmoid_gate * (1.0 + gate_value * (1.0 - sigmoid_gate))
    slopes = after(jnp.concatenate([to_gate, gate_value * sigmoid_gate], axis=0))
    both_units = after(
        jnp.concatenate(
            [jnp.concatenate([a, b], axis=1) for a, b in zip(mine[1:], theirs[1:])], axis=0
        )
    )

    right, left = after((right, left), slopes, both_units)
    grad_hidden = jnp.concatenate(
        [part + a + b for part, a, b in zip(parts(0), right, left)], axis=0
    )

    both = (jnp.concatenate([grad_hidden, grad_hidden], axis=0) * slopes).astype(BF16)
    start = jnp.where(xl == core, 0, block)
    size = (1, 1, block, output_rows.shape[3])
    lanes = size[3] // 2

    def kept_and_sent(pairs):
        kept = [dot(pair[0], both_units, 0, 0) for pair in pairs]
        out = [dot(pair[1], both_units, 0, 0).astype(BF16) for pair in pairs]
        return jnp.stack(kept), jnp.stack(out)

    def core_sum(kept, out):
        return kept + shift(out, "core", 2, 1).astype(F32)

    def halves(value):
        return value[:, :block], value[:, block:]

    def input_at(by):
        return lax.dynamic_index_in_dim(input_rows, (z + by) % 8, 0, keepdims=False)

    def weights_of(values, by, total=None):
        for value, k in zip(values, by):
            term = dot(value, input_at(k), 1, 0)
            total = after(term if total is None else total + term)
        return total

    def next_pair(pair, *others):
        return after((shift(pair[0], "z", 8, 1), shift(pair[1], "z", 8, -1)), *others)

    partial_down = None
    for j, value in enumerate(hidden_blocks):
        rows = lax.dynamic_slice(output_rows, place(j - z) + (start, 0), size).reshape(size[2:])
        term = dot(value, rows, 0, 0)
        partial_down = after(term if partial_down is None else partial_down + term)
    keep_down, give_down = partial_down[:, :lanes], partial_down[:, lanes:].astype(BF16)

    one = next_pair((both, both), keep_down, give_down)
    first = kept_and_sent([halves(value) for value in (both, one[1], one[0])])
    total = weights_of((both,), (0,))
    two = next_pair(one)
    first = core_sum(*first)
    second = kept_and_sent([halves(value) for value in (two[1], two[0])])
    total = weights_of((one[1], one[0]), (1, 7), total)
    grad_down = (keep_down + shift(give_down, "xl", 2, 1).astype(F32)) * factor
    three = next_pair(two, first, second, total, grad_down)
    third = kept_and_sent([halves(value) for value in (three[1], three[0])])
    late = tuple(jnp.concatenate(pair, axis=0) for pair in zip(second, third))
    total = weights_of((two[1], two[0], three[1], three[0]), (2, 6, 3, 5), total)
    far = (shift(three[0][:, :block], "z", 8, 1), shift(three[1][:, block:], "z", 8, -1))
    early = first
    far, early, late, total = after((far, early, late, total))
    last = kept_and_sent([far])
    late = core_sum(*(jnp.concatenate(pair, axis=0) for pair in zip(late, last)))
    summed = jnp.concatenate([early, late], axis=0)
    total = (total + dot(jnp.concatenate(far, axis=1), input_at(4), 1, 0)) * factor
    keep, give = total[:, :lanes], total[:, lanes:].astype(BF16)
    summed, give = after((summed, give))
    got = shift(give, "xl", 2, 1).astype(F32)

    def toward(xr, yr):
        by = (((xh + xr) % 2) * 4 + (y + yr) % 4 - z) % 8
        slot = jnp.maximum(0, 2 * jnp.minimum(by, 8 - by) - 1 + (by > 4))
        return lax.dynamic_slice_in_dim(summed, slot, 1, 0)

    def toward_y(yr):
        return jnp.concatenate([toward(0, yr), toward(1, yr)], axis=0)

    summed = (
        toward_y(0)
        + sent(toward_y(1), "y", 4, 1)
        + sent(toward_y(3), "y", 4, -1)
        + sent(toward_y(2), "y", 4, 2)
    )
    level, beyond = summed[0, :, lanes:], summed[1, :, lanes:]
    arrived = (
        sent(jnp.where(is_first, level, beyond), X, 4, 1),
        sent(jnp.where(is_first, beyond, level), X, 4, -1),
        sent(summed[1, :, :lanes], X, 4, 2),
    )

    def ordered(rows):
        return jnp.where(
            is_first,
            jnp.concatenate([keep[rows], got[rows]], axis=0),
            jnp.concatenate([got[rows], keep[rows]], axis=0),
        )

    grad_gate, grad_up = ordered(slice(0, units)), ordered(slice(units, 2 * units))
    arrived, grad_gate, grad_up = after((arrived, grad_gate, grad_up))
    grad_input = summed[0, :, :lanes] + sum(arrived)
    return grad_input, grad_gate, grad_up, grad_down


def solution(mesh):
    fine = Mesh(mesh.devices.reshape(2, 4, 2, 8, 2), ("xh", "y", "core", "z", "xl"))
    rows_cols = P(("xh", "y", "core"), ("z", "xl"))
    cols_rows = P(("z", "xl"), ("xh", "y", "core"))
    return jax.shard_map(
        shards,
        mesh=fine,
        in_specs=(rows_cols, rows_cols, cols_rows, cols_rows, rows_cols, rows_cols, rows_cols),
        out_specs=(rows_cols,) * 4,
        check_vma=False,
    )
```
